32 devices in a mesh: cube: 8 (over z, y), blk: 4 (over x, core).
Axes of the slice: x: 2, y: 2, z: 4, core: 2. Of those that a mesh axis runs over, the one named last changes fastest.
Arguments:
- rhs_root: bfloat16 [1, 10240, 128], P(None, 'blk'), may hold values from -6 to 6
- rhs_mid: bfloat16 [2, 10240, 128], P(None, 'blk'), may hold values from -6 to 6
- rhs_leaf: bfloat16 [4, 10240, 128], P(None, 'blk'), may hold values from -6 to 6
- pivot_root: bfloat16 [2, 10240, 10240], P(None, 'cube', 'blk'), may hold values from -0.0625 to 0.0625
- pivot_mid: bfloat16 [2, 20480, 10240], P(None, 'cube', 'blk'), may hold values from -0.0625 to 0.0625
- pivot_leaf: bfloat16 [2, 40960, 10240], P(None, 'cube', 'blk'), may hold values from -0.0625 to 0.0625
- coupling_mid: bfloat16 [2, 2560, 10240], P(None, 'cube', 'blk'), may hold values from -0.0625 to 0.0625
- coupling_leaf: bfloat16 [2, 5120, 10240], P(None, 'cube', 'blk'), may hold values from -0.0625 to 0.0625
- front_blocks: int32 [7], replicated, may hold values from 40 to 80, as said below
- child_map: int32 [6, 10], replicated, may hold values from 0 to 79
Outputs:
- solution_root: bfloat16 [4, 2560, 128], P('blk', 'cube')
- solution_mid: bfloat16 [4, 5120, 128], P('blk', 'cube')
- solution_leaf: bfloat16 [4, 10240, 128], P('blk', 'cube')
The draws below stay inside these ranges and needn't reach their ends.
Inputs may be any that keep to these rules, and one draw needn't show every extreme that they name: `front_blocks`: entry 0 is the root, entries 1 and 2 the level-1 fronts, 3 to 6 the level-2 fronts; at least one front is full in every draw. `child_map`: rows 0 and 1 belong to the level-1 fronts, row 2 + q to level-2 front q; targets may repeat within and across children.
All inputs are finite; a program needn't handle non-finite values.
Results may differ from the reference program's by a relative error of at most 0.013.
Values may be sent and summed in bfloat16 or wider, within the bound.
A program may use at most 192 MiB of HBM per device.

```python
import jax
import jax.numpy as jnp

SEPARATOR = 10240
UPDATES = 1280
BLOCK_ROWS = 128
SOURCES = 64
N_BLK = 4


def draw_front_blocks(key, part):
    first, second = jax.random.split(key)
    largest = SEPARATOR // BLOCK_ROWS
    values = jax.random.randint(first, (7,), largest // 2, largest + 1)
    chosen = jax.random.randint(second, (), 0, 7)
    return jnp.where(jnp.arange(7) == chosen, largest, values).astype(jnp.int32)


def place_ends(array, own_key, smallest, high):
    extent = array.shape
    spot = [jax.random.randint(jax.random.fold_in(own_key, axis), (), 0, extent[axis]) for axis in range(len(extent))]
    array = array.at[tuple(spot)].set(smallest)
    longest = extent.index(max(extent))
    spot[longest] = (spot[longest] + 1) % extent[longest]
    return array.at[tuple(spot)].set(high)


def levels(stream_key, extent, cuts, low, top_value):
    def one(dim, shards_of):
        heights = jax.random.uniform(jax.random.fold_in(jax.random.fold_in(stream_key, 6), dim), (shards_of,), jnp.float32, low / len(cuts), top_value / len(cuts))
        return jnp.repeat(jnp.exp(heights), extent[dim] // shards_of).reshape((-1,) + (1,) * (len(extent) - dim - 1))

    factor_of = one(*cuts[0])
    for cut in cuts[1:]:
        factor_of = factor_of * one(*cut)
    return factor_of


def normal_values(rng, dims, spread, bound, cuts=(), held_as=jnp.bfloat16):
    result = spread * jax.random.normal(rng, dims, jnp.float32)
    if cuts:
        result = result * levels(rng, dims, cuts, -0.22, 0.18)
    return jnp.clip(result, -bound, bound).astype(held_as)


def setup_inputs(seed: int = 0) -> dict:
    keys = jax.random.split(jax.random.key(seed), 11)
    rhs_root = normal_values(keys[0], (1, SEPARATOR, 2 * SOURCES), 1.0, 6.0, ((1, 4),))
    rhs_mid = normal_values(keys[1], (2, SEPARATOR, 2 * SOURCES), 1.0, 6.0, ((1, 4),))
    rhs_leaf = normal_values(keys[2], (4, SEPARATOR, 2 * SOURCES), 1.0, 6.0, ((1, 4),))
    pivot_root = normal_values(keys[3], (2, SEPARATOR, SEPARATOR), SEPARATOR ** -0.5, 0.0625, ((1, 8), (2, 4)))
    pivot_mid = normal_values(keys[4], (2, 2 * SEPARATOR, SEPARATOR), SEPARATOR ** -0.5, 0.0625, ((1, 8), (2, 4)))
    pivot_leaf = normal_values(keys[5], (2, 4 * SEPARATOR, SEPARATOR), SEPARATOR ** -0.5, 0.0625, ((1, 8), (2, 4)))
    coupling_mid = normal_values(keys[6], (2, 2 * UPDATES, SEPARATOR), SEPARATOR ** -0.5, 0.0625, ((1, 8), (2, 4)))
    coupling_leaf = normal_values(keys[7], (2, 4 * UPDATES, SEPARATOR), SEPARATOR ** -0.5, 0.0625, ((1, 8), (2, 4)))
    front_blocks = draw_front_blocks(jax.random.fold_in(keys[10], 71), 0)
    child_map = place_ends(jax.random.randint(keys[9], (6, UPDATES // BLOCK_ROWS), 0, SEPARATOR // BLOCK_ROWS), jax.random.fold_in(keys[9], 1), 0, (SEPARATOR // BLOCK_ROWS) - 1).astype(jnp.int32)
    return dict(rhs_root=rhs_root, rhs_mid=rhs_mid, rhs_leaf=rhs_leaf, pivot_root=pivot_root, pivot_mid=pivot_mid, pivot_leaf=pivot_leaf, coupling_mid=coupling_mid, coupling_leaf=coupling_leaf, front_blocks=front_blocks, child_map=child_map)


def rotate_parts(vec):
    half = vec.shape[1] // 2
    return jnp.concatenate([-vec[:, half:], vec[:, :half]], axis=1)


def complex_apply(matrix, vec):
    first = jnp.dot(matrix[0], vec, preferred_element_type=jnp.float32)
    second = jnp.dot(matrix[1], rotate_parts(vec), preferred_element_type=jnp.float32)
    return first + second


def complex_apply_t(matrix, vec):
    first = jnp.dot(matrix[0].T, vec, preferred_element_type=jnp.float32)
    second = jnp.dot(matrix[1].T, rotate_parts(vec), preferred_element_type=jnp.float32)
    return first + second


def target_rows(targets):
    offsets = jnp.arange(BLOCK_ROWS, dtype=jnp.int32)
    return (targets[:, None].astype(jnp.int32) * BLOCK_ROWS + offsets[None, :]).reshape(-1)


def spread_update(update, targets):
    empty = jnp.zeros((SEPARATOR, 2 * SOURCES), jnp.float32)
    return empty.at[target_rows(targets)].add(update.astype(jnp.float32))


def mask_of(front_blocks, index):
    rows = jnp.arange(SEPARATOR, dtype=jnp.int32)
    return (rows < front_blocks[index] * BLOCK_ROWS).astype(jnp.float32)[:, None]


def forward_front(pivot, coupling, gathered, mask):
    masked = (mask * gathered).astype(jnp.bfloat16)
    solved = (mask * complex_apply(pivot, masked)).astype(jnp.bfloat16)
    update = None
    if coupling is not None:
        update = complex_apply(coupling, masked).astype(jnp.bfloat16)
    return solved, update


def layout(fronts):
    stacked = jnp.stack(fronts)
    count = stacked.shape[0]
    shaped = stacked.reshape(count, N_BLK, SEPARATOR // N_BLK, 2 * SOURCES)
    return shaped.transpose(1, 0, 2, 3).reshape(N_BLK, count * SEPARATOR // N_BLK, 2 * SOURCES)


def reference(rhs_root, rhs_mid, rhs_leaf, pivot_root, pivot_mid, pivot_leaf, coupling_mid, coupling_leaf, front_blocks, child_map):
    sep = SEPARATOR
    upd = UPDATES
    solved_leaf, update_leaf = [], []
    for front in range(4):
        pivot = pivot_leaf[:, front * sep:(front + 1) * sep, :]
        coupling = coupling_leaf[:, front * upd:(front + 1) * upd, :]
        gathered = rhs_leaf[front].astype(jnp.float32)
        solved, update = forward_front(pivot, coupling, gathered, mask_of(front_blocks, 3 + front))
        solved_leaf.append(solved)
        update_leaf.append(update)
    solved_mid, update_mid = [], []
    for front in range(2):
        pivot = pivot_mid[:, front * sep:(front + 1) * sep, :]
        coupling = coupling_mid[:, front * upd:(front + 1) * upd, :]
        gathered = rhs_mid[front].astype(jnp.float32)
        gathered = gathered - spread_update(update_leaf[2 * front], child_map[2 + 2 * front])
        gathered = gathered - spread_update(update_leaf[2 * front + 1], child_map[3 + 2 * front])
        solved, update = forward_front(pivot, coupling, gathered, mask_of(front_blocks, 1 + front))
        solved_mid.append(solved)
        update_mid.append(update)
    gathered = rhs_root[0].astype(jnp.float32)
    gathered = gathered - spread_update(update_mid[0], child_map[0]) - spread_update(update_mid[1], child_map[1])
    mask_root = mask_of(front_blocks, 0)
    solved_root, unused = forward_front(pivot_root, None, gathered, mask_root)
    answer_root = (mask_root * complex_apply_t(pivot_root, solved_root)).astype(jnp.bfloat16)
    answer_mid = []
    for front in range(2):
        pivot = pivot_mid[:, front * sep:(front + 1) * sep, :]
        coupling = coupling_mid[:, front * upd:(front + 1) * upd, :]
        pulled = answer_root[target_rows(child_map[front])]
        term = complex_apply_t(pivot, solved_mid[front]) - complex_apply_t(coupling, pulled)
        answer_mid.append((mask_of(front_blocks, 1 + front) * term).astype(jnp.bfloat16))
    answer_leaf = []
    for front in range(4):
        pivot = pivot_leaf[:, front * sep:(front + 1) * sep, :]
        coupling = coupling_leaf[:, front * upd:(front + 1) * upd, :]
        pulled = answer_mid[front // 2][target_rows(child_map[2 + front])]
        term = complex_apply_t(pivot, solved_leaf[front]) - complex_apply_t(coupling, pulled)
        answer_leaf.append((mask_of(front_blocks, 3 + front) * term).astype(jnp.bfloat16))
    return (layout([answer_root]), layout(answer_mid), layout(answer_leaf))
```

```python
import jax
import jax.numpy as jnp
from jax import lax
from jax.experimental import pallas as pl
from jax.experimental.pallas import tpu as pltpu
from jax.sharding import PartitionSpec as P

SEPARATOR = 10240
BLOCK_ROWS = 128


def swapped(value, axis, distance):
    return lax.ppermute(value, axis, [(i, i ^ 1 << distance) for i in range(lax.axis_size(axis))])


def rotate_parts(vec):
    half = vec.shape[1] // 2
    return jnp.concatenate([-vec[:, half:], vec[:, :half]], axis=1)


def complex_apply(matrix, vec):
    first = jnp.dot(matrix[0], vec, preferred_element_type=jnp.float32)
    second = jnp.dot(matrix[1], rotate_parts(vec), preferred_element_type=jnp.float32)
    return first + second


def complex_apply_t(matrix, vec):
    dims = (((0,), (0,)), ((), ()))
    first = lax.dot_general(matrix[0], vec, dims, preferred_element_type=jnp.float32)
    second = lax.dot_general(matrix[1], rotate_parts(vec), dims, preferred_element_type=jnp.float32)
    return first + second


def bit_set(cube_at, bit):
    return cube_at >> bit & 1 == 1


def gather_bits(piece, count, cube_at):
    for bit in range(count):
        other = swapped(piece, "cube", bit)
        upper = bit_set(cube_at, bit)
        piece = jnp.where(
            upper, jnp.concatenate([other, piece], 0), jnp.concatenate([piece, other], 0)
        )
    return piece


def swap_sum(value, bit):
    return swapped(value.astype(jnp.bfloat16), "cube", bit).astype(value.dtype)


def halve_bits(total, count, cube_at):
    for bit in reversed(range(count)):
        rows = total.shape[0] // 2
        lower = total[:rows]
        higher = total[rows:]
        upper = bit_set(cube_at, bit)
        sent = jnp.where(upper, lower, higher)
        kept = jnp.where(upper, higher, lower)
        total = kept + swap_sum(sent, bit)
    return total


def blk_total(value):
    return lax.psum(value, "blk")


def row_mask(start, count, limit):
    rows = start + jnp.arange(count, dtype=jnp.int32)
    return (rows < limit).astype(jnp.float32)[:, None]


def extend_add(gathered, targets, first_block, slice_blocks):
    blocks = gathered.reshape(targets.shape[0], BLOCK_ROWS, gathered.shape[1])
    slots = jnp.arange(slice_blocks, dtype=jnp.int32)
    placing = (targets[None, :] - first_block == slots[:, None]).astype(jnp.bfloat16)
    summed = jnp.einsum("ti,ird->trd", placing, blocks, preferred_element_type=jnp.float32)
    return summed.reshape(slice_blocks * BLOCK_ROWS, gathered.shape[1])


def pick_rows(parent_slice, targets, rows, first_row):
    block_of = rows // BLOCK_ROWS
    table = (block_of[:, None] == jnp.arange(targets.shape[0], dtype=jnp.int32)[None, :]).astype(
        jnp.int32
    )
    target_block = jnp.sum(table * targets[None, :], axis=1)
    where_row = target_block * BLOCK_ROWS + rows % BLOCK_ROWS - first_row
    inside = (where_row >= 0) & (where_row < parent_slice.shape[0])
    values = parent_slice[jnp.clip(where_row, 0, parent_slice.shape[0] - 1)].astype(jnp.float32)
    return jnp.where(inside[:, None], values, 0.0)


def forward_front(pivot, coupling, gathered, column_mask, solved_mask):
    masked = (column_mask * gathered).astype(jnp.bfloat16)
    own_rows = pivot.shape[1]
    if coupling is None:
        sums = blk_total(complex_apply(pivot, masked))
        return ((solved_mask * sums).astype(jnp.bfloat16), None)
    both = jnp.concatenate([complex_apply(pivot, masked), complex_apply(coupling, masked)], 0)
    sums = blk_total(both)
    solved = (solved_mask * sums[:own_rows]).astype(jnp.bfloat16)
    return (solved, sums[own_rows:].astype(jnp.bfloat16))


def per_device_plain(
    rhs_root,
    rhs_mid,
    rhs_leaf,
    pivot_root,
    pivot_mid,
    pivot_leaf,
    coupling_mid,
    coupling_leaf,
    front_blocks,
    child_map,
):
    cube_n = lax.axis_size("cube")
    blk_n = lax.axis_size("blk")
    cube_at = lax.axis_index("cube")
    blk_at = lax.axis_index("blk")
    slice_rows = SEPARATOR // blk_n
    slice_blocks = slice_rows // BLOCK_ROWS
    first_row = blk_at * slice_rows
    first_block = blk_at * slice_blocks
    group_mid = cube_n // 2
    group_leaf = cube_n // 4
    bits_root = cube_n.bit_length() - 1
    bits_mid = bits_root - 1
    bits_leaf = bits_root - 2
    front_mid = cube_at // group_mid
    place_mid = cube_at % group_mid
    front_leaf = cube_at // group_leaf
    place_leaf = cube_at % group_leaf
    size_root = front_blocks[0] * BLOCK_ROWS
    size_mid = front_blocks[1 + front_mid] * BLOCK_ROWS
    size_leaf = front_blocks[3 + front_leaf] * BLOCK_ROWS
    column_leaf = row_mask(first_row, slice_rows, size_leaf)
    column_mid = row_mask(first_row, slice_rows, size_mid)
    column_root = row_mask(first_row, slice_rows, size_root)
    own_leaf = pivot_leaf.shape[1]
    gathered = lax.dynamic_index_in_dim(rhs_leaf, front_leaf, 0, keepdims=False).astype(jnp.float32)
    solved_leaf, update_leaf = forward_front(
        pivot_leaf,
        coupling_leaf,
        gathered,
        column_leaf,
        row_mask(place_leaf * own_leaf, own_leaf, size_leaf),
    )
    own_mid = pivot_mid.shape[1]
    arrived = gather_bits(update_leaf, bits_mid, cube_at)
    targets = lax.dynamic_slice_in_dim(child_map, 2 + 2 * front_mid, 2, 0).reshape(-1)
    gathered = lax.dynamic_index_in_dim(rhs_mid, front_mid, 0, keepdims=False).astype(jnp.float32)
    gathered = gathered - extend_add(arrived, targets, first_block, slice_blocks)
    solved_mid, update_mid = forward_front(
        pivot_mid,
        coupling_mid,
        gathered,
        column_mid,
        row_mask(place_mid * own_mid, own_mid, size_mid),
    )
    own_root = pivot_root.shape[1]
    arrived = gather_bits(update_mid, bits_root, cube_at)
    targets = child_map[0:2].reshape(-1)
    gathered = rhs_root[0].astype(jnp.float32) - extend_add(
        arrived, targets, first_block, slice_blocks
    )
    solved_root, unused = forward_front(
        pivot_root, None, gathered, column_root, row_mask(cube_at * own_root, own_root, size_root)
    )
    total = lax.psum(complex_apply_t(pivot_root, solved_root), "cube")
    full_root = (column_root * total).astype(jnp.bfloat16)
    piece_root = slice_rows // cube_n
    answer_root = lax.dynamic_slice_in_dim(full_root, cube_at * piece_root, piece_root, 0)
    update_rows_mid = coupling_mid.shape[1]
    rows = place_mid * update_rows_mid + jnp.arange(update_rows_mid, dtype=jnp.int32)
    targets = lax.dynamic_slice_in_dim(child_map, front_mid, 1, 0).reshape(-1)
    pulled = blk_total(pick_rows(full_root, targets, rows, first_row)).astype(jnp.bfloat16)
    term = complex_apply_t(pivot_mid, solved_mid) - complex_apply_t(coupling_mid, pulled)
    piece_mid = slice_rows // group_mid
    share = halve_bits(term, bits_mid, cube_at)
    answer_mid = (row_mask(first_row + place_mid * piece_mid, piece_mid, size_mid) * share).astype(
        jnp.bfloat16
    )
    full_mid = gather_bits(answer_mid, bits_mid, cube_at)
    update_rows_leaf = coupling_leaf.shape[1]
    rows = place_leaf * update_rows_leaf + jnp.arange(update_rows_leaf, dtype=jnp.int32)
    targets = lax.dynamic_slice_in_dim(child_map, 2 + front_leaf, 1, 0).reshape(-1)
    pulled = blk_total(pick_rows(full_mid, targets, rows, first_row)).astype(jnp.bfloat16)
    term = complex_apply_t(pivot_leaf, solved_leaf) - complex_apply_t(coupling_leaf, pulled)
    piece_leaf = slice_rows // group_leaf
    share = halve_bits(term, bits_leaf, cube_at)
    answer_leaf = (
        row_mask(first_row + place_leaf * piece_leaf, piece_leaf, size_leaf) * share
    ).astype(jnp.bfloat16)
    return (answer_root[None], answer_mid[None], answer_leaf[None])

MESH = pl.DeviceIdType.MESH
VMEM = pltpu.VMEM
TILE_ROWS = 256
SLOTS = 3


class Links:
    def __init__(self, cube_n, blk_n):
        self.cube_n = cube_n
        self.blk_n = blk_n
        self.cube = lax.axis_index("cube")
        self.blk = lax.axis_index("blk")
        self.used = 0

    def bind(self, send, recv):
        self.send = send
        self.recv = recv

    def start(self, src, dst, device):
        at = self.used
        self.used += 1
        copy = pltpu.make_async_remote_copy(
            src_ref=src,
            dst_ref=dst,
            send_sem=self.send.at[at],
            recv_sem=self.recv.at[at],
            device_id=device,
            device_id_type=MESH,
        )
        copy.start()
        return copy

    def cube_peer(self, group, step):
        place = lax.rem(self.cube, group)
        other = lax.rem(place + step, group)
        return other, (self.cube - place + other, self.blk)

    def blk_peer(self, step):
        other = lax.rem(self.blk + step, self.blk_n)
        return other, (self.cube, other)

    def core(self):
        return lax.rem(self.blk, 2)

    def chip(self):
        return self.blk // 2

    def core_peer(self):
        other = 1 - self.core()
        return other, (self.cube, self.chip() * 2 + other)

    def chip_peer(self):
        other = 1 - self.chip()
        return other, (self.cube, other * 2 + self.core())

    def barrier(self, group):
        barrier = pltpu.get_barrier_semaphore()
        peers = [self.blk_peer(k)[1] for k in range(1, self.blk_n)]
        peers += [self.cube_peer(group, k)[1] for k in range(1, group)]
        for peer in peers:
            pl.semaphore_signal(barrier, inc=1, device_id=peer, device_id_type=MESH)
        pl.semaphore_wait(barrier, len(peers))


def wait_all(copies):
    for copy in copies:
        copy.wait()


def f32(value):
    return value.astype(jnp.float32)


def bf16(value):
    return value.astype(jnp.bfloat16)


def update_chain(links, src, out, got, own, group):
    copies = []
    for k in range(1, links.blk_n):
        other, device = links.blk_peer(k)
        copies.append(links.start(src.at[other], got.at[k - 1], device))
    yield
    wait_all(copies)
    total = f32(src[links.blk])
    for k in range(1, links.blk_n):
        total = total + f32(got[k - 1])
    own[...] = bf16(total)
    place = lax.rem(links.cube, group)
    out[place, links.blk] = own[...]
    copies = []
    for k in range(1, group):
        other, device = links.cube_peer(group, k)
        copies.append(links.start(own, out.at[place, links.blk], device))
    yield
    wait_all(copies)
    mine = out.at[:, links.blk]
    other, device = links.chip_peer()
    copies = [links.start(mine, mine, device)]
    other, device = links.core_peer()
    copies.append(links.start(mine, mine, device))
    yield
    wait_all(copies)
    across = out.at[:, (1 - links.chip()) * 2 + links.core()]
    copy = links.start(across, across, device)
    yield
    copy.wait()


def sum_chain(links, src, out, got_core, half, got_chip, own):
    other, device = links.core_peer()
    copy = links.start(src.at[:, other], got_core, device)
    yield
    copy.wait()
    half[...] = bf16(f32(src[:, links.core()]) + f32(got_core[...]))
    other, device = links.chip_peer()
    copy = links.start(half.at[other], got_chip, device)
    yield
    copy.wait()
    own[...] = bf16(f32(half[links.chip()]) + f32(got_chip[...]))
    out[links.chip(), links.core()] = own[...]
    place = out.at[links.chip(), links.core()]
    copy = links.start(own, place, device)
    other, device = links.core_peer()
    near = links.start(own, place, device)
    yield
    copy.wait()
    near.wait()
    place = out.at[1 - links.chip(), links.core()]
    copy = links.start(place, place, device)
    yield
    copy.wait()


def scatter_chain(links, src, out, got, group):
    copies = []
    for k in range(1, group):
        other, device = links.cube_peer(group, k)
        copies.append(links.start(src.at[other], got.at[k - 1], device))
    yield
    wait_all(copies)
    total = f32(src[lax.rem(links.cube, group)])
    for k in range(1, group):
        total = total + f32(got[k - 1])
    out[...] = bf16(total)


def pick_chain(links, src, out, got, mid, group, rest):
    yield from scatter_chain(links, src, mid, got, group)
    yield from sum_chain(links, mid, out, *rest)


def vm(*shape):
    return VMEM(shape, jnp.bfloat16)


def sum_scratch(rows):
    return [vm(2, rows, 128), vm(2, rows, 128), vm(rows, 128), vm(rows, 128)]


def chain_plan(kind, src, group):
    shape = src.shape
    if kind == "update":
        n, rows = shape[0], shape[1]
        return (
            (group, n, rows, 128),
            [vm(n - 1, rows, 128), vm(rows, 128)],
            n + group + 2,
            lambda L, s, o, t: update_chain(L, s, o, t[0], t[1], group),
        )
    if kind == "sum":
        return shape, sum_scratch(shape[2]), 5, lambda L, s, o, t: sum_chain(L, s, o, *t)
    if kind == "scatter":
        return (
            shape[1:],
            [vm(group - 1, *shape[1:])],
            group,
            lambda L, s, o, t: scatter_chain(L, s, o, t[0], group),
        )
    return (
        shape[1:],
        [vm(group - 1, *shape[1:]), vm(*shape[1:])] + sum_scratch(shape[3]),
        group + 5,
        lambda L, s, o, t: pick_chain(L, s, o, t[0], t[1], group, t[2:]),
    )


def exchange(chains, work, collective_id, cube_n, blk_n):
    plans = [chain_plan(kind, array, group) for kind, array, group in chains]
    largest = max(group for _, _, group in chains)
    n_chains = len(chains)
    arrays = [array for _, array, _ in chains]
    outs = [jax.ShapeDtypeStruct(plan[0], jnp.bfloat16) for plan in plans]
    n_copies = sum(plan[2] for plan in plans)
    scratch = [pltpu.SemaphoreType.DMA((n_copies,)), pltpu.SemaphoreType.DMA((n_copies,))]
    for plan in plans:
        scratch += plan[1]
    in_specs = [pl.BlockSpec(memory_space=VMEM)] * n_chains
    cost = None
    if work is not None:
        mode, matrix, vectors, first, rows = work
        width = matrix.shape[2]
        steps = rows // TILE_ROWS
        arrays += [matrix, vectors]
        in_specs += [pl.BlockSpec(memory_space=pl.ANY), pl.BlockSpec(memory_space=VMEM)]
        if mode == "f":
            outs.append(jax.ShapeDtypeStruct((rows, 128), jnp.bfloat16))
        else:
            outs.append(jax.ShapeDtypeStruct((128, width), jnp.float32))
        scratch += [VMEM((SLOTS, 2, TILE_ROWS, width), matrix.dtype), pltpu.SemaphoreType.DMA((SLOTS,))]

    def kernel(*refs):
        n_in = len(arrays)
        srcs, refs = refs[:n_in], refs[n_in:]
        dsts, refs = refs[: len(outs)], refs[len(outs) :]
        links = Links(cube_n, blk_n)
        links.bind(refs[0], refs[1])
        at = 2
        running = []
        for i, plan in enumerate(plans):
            count = len(plan[1])
            running.append(plan[3](links, srcs[i], dsts[i], refs[at : at + count]))
            at += count

        if work is not None:
            a_ref, v_ref = srcs[n_chains:]
            y_ref = dsts[n_chains]
            buf, sems = refs[at], refs[at + 1]

            def tile(i):
                slot = lax.rem(i, SLOTS)
                return pltpu.make_async_copy(
                    a_ref.at[:, pl.ds(first + i * TILE_ROWS, TILE_ROWS), :], buf.at[slot], sems.at[slot]
                )

            for i in range(min(SLOTS - 1, steps)):
                tile(i).start()
            if mode != "f":
                y_ref[...] = jnp.zeros_like(y_ref)

            def step(i):
                @pl.when(i + SLOTS - 1 < steps)
                def _():
                    tile(i + SLOTS - 1).start()

                tile(i).wait()
                slot = lax.rem(i, SLOTS)
                at_row = pl.ds(pl.multiple_of(i * TILE_ROWS, TILE_ROWS), TILE_ROWS)
                if mode == "f":
                    total = jnp.dot(buf[slot, 0], v_ref[0], preferred_element_type=jnp.float32)
                    total += jnp.dot(buf[slot, 1], v_ref[1], preferred_element_type=jnp.float32)
                    y_ref[at_row, :] = bf16(total)
                else:
                    y_ref[...] += jnp.dot(
                        v_ref[0, i], buf[slot, 0], preferred_element_type=jnp.float32
                    ) + jnp.dot(v_ref[1, i], buf[slot, 1], preferred_element_type=jnp.float32)

        links.barrier(largest)

        def advance():
            alive = []
            for chain in running:
                try:
                    next(chain)
                    alive.append(chain)
                except StopIteration:
                    pass
            running[:] = alive

        if work is not None:
            parts = 5
            cuts = [steps * j // parts for j in range(parts + 1)]
            for lo, hi in zip(cuts, cuts[1:]):
                advance()
                if hi > lo:
                    pl.loop(lo, hi)(step)
        while running:
            advance()

    results = pl.pallas_call(
        kernel,
        out_shape=outs,
        in_specs=in_specs,
        out_specs=[pl.BlockSpec(memory_space=VMEM)] * len(outs),
        scratch_shapes=scratch,
        compiler_params=pltpu.CompilerParams(
            collective_id=collective_id, has_side_effects=True, vmem_limit_bytes=60 * 1024 * 1024
        ),
    )(*arrays)
    return results


def both_parts(vec):
    return jnp.stack([vec, rotate_parts(vec)])


def tiles_t(vec):
    parts = both_parts(vec)
    return parts.reshape(2, -1, TILE_ROWS, vec.shape[1]).transpose(0, 1, 3, 2)


def pick_blocks(piece, targets, first_block):
    blocks = piece.reshape(-1, BLOCK_ROWS, piece.shape[1])
    slots = jnp.arange(blocks.shape[0], dtype=jnp.int32)
    placing = (targets[:, None] - first_block == slots[None, :]).astype(jnp.bfloat16)
    picked = jnp.einsum("it,trd->ird", placing, blocks, preferred_element_type=jnp.float32)
    return bf16(picked).reshape(-1, piece.shape[1])


def per_device_fast(
    rhs_root,
    rhs_mid,
    rhs_leaf,
    pivot_root,
    pivot_mid,
    pivot_leaf,
    coupling_mid,
    coupling_leaf,
    front_blocks,
    child_map,
):
    cube_n = lax.axis_size("cube")
    blk_n = lax.axis_size("blk")
    cube_at = lax.axis_index("cube")
    blk_at = lax.axis_index("blk")
    slice_rows = rhs_root.shape[1]
    slice_blocks = slice_rows // BLOCK_ROWS
    first_row = blk_at * slice_rows
    first_block = blk_at * slice_blocks
    group_mid = cube_n // 2
    group_leaf = cube_n // 4
    front_mid = cube_at // group_mid
    place_mid = cube_at % group_mid
    front_leaf = cube_at // group_leaf
    place_leaf = cube_at % group_leaf
    size_root = front_blocks[0] * BLOCK_ROWS
    size_mid = front_blocks[1 + front_mid] * BLOCK_ROWS
    size_leaf = front_blocks[3 + front_leaf] * BLOCK_ROWS
    column_leaf = row_mask(first_row, slice_rows, size_leaf)
    column_mid = row_mask(first_row, slice_rows, size_mid)
    column_root = row_mask(first_row, slice_rows, size_root)
    own_leaf = pivot_leaf.shape[1]
    own_mid = pivot_mid.shape[1]
    own_root = pivot_root.shape[1]
    half_leaf = own_leaf // 2

    def by_blk(value):
        return value.reshape(blk_n, -1, 128)

    def by_core(value):
        return value.reshape(2, 2, -1, 128)

    def run(chains, work, collective_id):
        return exchange(chains, work, collective_id, cube_n, blk_n)

    gathered = f32(lax.dynamic_index_in_dim(rhs_leaf, front_leaf, 0, keepdims=False))
    masked_leaf = bf16(column_leaf * gathered)
    update = bf16(complex_apply(coupling_leaf, masked_leaf))
    vec_leaf = both_parts(masked_leaf)
    arrived, solved_low = run(
        [("update", by_blk(update), group_mid)], ("f", pivot_leaf, vec_leaf, 0, half_leaf), 0
    )
    targets = lax.dynamic_slice_in_dim(child_map, 2 + 2 * front_mid, 2, 0).reshape(-1)
    gathered = f32(lax.dynamic_index_in_dim(rhs_mid, front_mid, 0, keepdims=False))
    gathered = gathered - extend_add(arrived.reshape(-1, 128), targets, first_block, slice_blocks)
    masked_mid = bf16(column_mid * gathered)
    update = bf16(complex_apply(coupling_mid, masked_mid))
    arrived, solved_mid = run(
        [("update", by_blk(update), cube_n)],
        ("f", pivot_mid, both_parts(masked_mid), 0, own_mid),
        1,
    )
    targets = child_map[0:2].reshape(-1)
    gathered = f32(rhs_root[0]) - extend_add(
        arrived.reshape(-1, 128), targets, first_block, slice_blocks
    )
    masked_root = bf16(column_root * gathered)
    solved_root = bf16(complex_apply(pivot_root, masked_root))
    solved_root, solved_mid, solved_high = run(
        [("sum", by_core(solved_root), 1), ("sum", by_core(solved_mid), 1)],
        ("f", pivot_leaf, vec_leaf, half_leaf, own_leaf - half_leaf),
        2,
    )
    solved_root = bf16(
        row_mask(cube_at * own_root, own_root, size_root) * f32(solved_root.reshape(-1, 128))
    )
    solved_mid = bf16(
        row_mask(place_mid * own_mid, own_mid, size_mid) * f32(solved_mid.reshape(-1, 128))
    )
    solved_leaf = jnp.concatenate([solved_low, solved_high], 0)
    part_root = bf16(column_root * complex_apply_t(pivot_root, solved_root))
    targets = child_map[0:2].reshape(-1)
    picked = pick_blocks(part_root, targets, first_block)
    pulled, solved_leaf, term = run(
        [
            ("pick", picked.reshape(cube_n, 2, 2, -1, 128), cube_n),
            ("sum", by_core(solved_leaf), 1),
        ],
        ("t", pivot_mid, tiles_t(solved_mid), 0, own_mid),
        3,
    )
    solved_leaf = bf16(
        row_mask(place_leaf * own_leaf, own_leaf, size_leaf) * f32(solved_leaf.reshape(-1, 128))
    )
    term = term.T - complex_apply_t(coupling_mid, pulled.reshape(-1, 128))
    part_mid = bf16(column_mid * term)
    targets = lax.dynamic_slice_in_dim(child_map, 2 + 2 * front_mid, 2, 0).reshape(-1)
    picked = pick_blocks(part_mid, targets, first_block)
    pulled, answer_root, term = run(
        [
            ("pick", picked.reshape(group_mid, 2, 2, -1, 128), group_mid),
            ("scatter", part_root.reshape(cube_n, -1, 128), cube_n),
        ],
        ("t", pivot_leaf, tiles_t(solved_leaf), 0, own_leaf),
        4,
    )
    term = term.T - complex_apply_t(coupling_leaf, pulled.reshape(-1, 128))
    part_leaf = bf16(column_leaf * term)
    answer_leaf, answer_mid = run(
        [
            ("scatter", part_leaf.reshape(group_leaf, -1, 128), group_leaf),
            ("scatter", part_mid.reshape(group_mid, -1, 128), group_mid),
        ],
        None,
        5,
    )
    return (answer_root[None], answer_mid[None], answer_leaf[None])


def per_device(*args):
    cube_n = lax.axis_size("cube")
    blk_n = lax.axis_size("blk")
    pivot_root, pivot_mid, pivot_leaf, coupling_mid = args[3], args[4], args[5], args[6]
    fits = (
        blk_n == 4
        and cube_n % 4 == 0
        and args[0].shape[2] == 128
        and coupling_mid.shape[1] % (16 * blk_n) == 0
        and pivot_root.shape[1] % (16 * blk_n) == 0
        and pivot_mid.shape[1] % TILE_ROWS == 0
        and pivot_leaf.shape[1] % (2 * TILE_ROWS) == 0
    )
    return per_device_fast(*args) if fits else per_device_plain(*args)


def solution(mesh):
    in_specs = (
        P(None, "blk", None),
        P(None, "blk", None),
        P(None, "blk", None),
        P(None, "cube", "blk"),
        P(None, "cube", "blk"),
        P(None, "cube", "blk"),
        P(None, "cube", "blk"),
        P(None, "cube", "blk"),
        P(),
        P(),
    )
    out_specs = (P("blk", "cube", None), P("blk", "cube", None), P("blk", "cube", None))
    return jax.shard_map(
        per_device, mesh=mesh, in_specs=in_specs, out_specs=out_specs, check_vma=False
    )
```

```python
import jax
import jax.numpy as jnp
from jax import lax
from jax.experimental import pallas as pl
from jax.experimental.pallas import tpu as pltpu
from jax.sharding import PartitionSpec as P

SEPARATOR = 10240
BLOCK_ROWS = 128


def swapped(value, axis, distance):
    return lax.ppermute(value, axis, [(i, i ^ 1 << distance) for i in range(lax.axis_size(axis))])


def rotate_parts(vec):
    half = vec.shape[1] // 2
    return jnp.concatenate([-vec[:, half:], vec[:, :half]], axis=1)


def complex_apply(matrix, vec):
    first = jnp.dot(matrix[0], vec, preferred_element_type=jnp.float32)
    second = jnp.dot(matrix[1], rotate_parts(vec), preferred_element_type=jnp.float32)
    return first + second


def complex_apply_t(matrix, vec):
    dims = (((0,), (0,)), ((), ()))
    first = lax.dot_general(matrix[0], vec, dims, preferred_element_type=jnp.float32)
    second = lax.dot_general(matrix[1], rotate_parts(vec), dims, preferred_element_type=jnp.float32)
    return first + second


def bit_set(cube_at, bit):
    return cube_at >> bit & 1 == 1


def gather_bits(piece, count, cube_at):
    for bit in range(count):
        other = swapped(piece, "cube", bit)
        upper = bit_set(cube_at, bit)
        piece = jnp.where(
            upper, jnp.concatenate([other, piece], 0), jnp.concatenate([piece, other], 0)
        )
    return piece


def swap_sum(value, bit):
    return swapped(value.astype(jnp.bfloat16), "cube", bit).astype(value.dtype)


def halve_bits(total, count, cube_at):
    for bit in reversed(range(count)):
        rows = total.shape[0] // 2
        lower = total[:rows]
        higher = total[rows:]
        upper = bit_set(cube_at, bit)
        sent = jnp.where(upper, lower, higher)
        kept = jnp.where(upper, higher, lower)
        total = kept + swap_sum(sent, bit)
    return total


def blk_total(value):
    return lax.psum(value, "blk")


def row_mask(start, count, limit):
    rows = start + jnp.arange(count, dtype=jnp.int32)
    return (rows < limit).astype(jnp.float32)[:, None]


def extend_add(gathered, targets, first_block, slice_blocks):
    blocks = gathered.reshape(targets.shape[0], BLOCK_ROWS, gathered.shape[1])
    slots = jnp.arange(slice_blocks, dtype=jnp.int32)
    placing = (targets[None, :] - first_block == slots[:, None]).astype(jnp.bfloat16)
    summed = jnp.einsum("ti,ird->trd", placing, blocks, preferred_element_type=jnp.float32)
    return summed.reshape(slice_blocks * BLOCK_ROWS, gathered.shape[1])


def pick_rows(parent_slice, targets, rows, first_row):
    block_of = rows // BLOCK_ROWS
    table = (block_of[:, None] == jnp.arange(targets.shape[0], dtype=jnp.int32)[None, :]).astype(
        jnp.int32
    )
    target_block = jnp.sum(table * targets[None, :], axis=1)
    where_row = target_block * BLOCK_ROWS + rows % BLOCK_ROWS - first_row
    inside = (where_row >= 0) & (where_row < parent_slice.shape[0])
    values = parent_slice[jnp.clip(where_row, 0, parent_slice.shape[0] - 1)].astype(jnp.float32)
    return jnp.where(inside[:, None], values, 0.0)


def forward_front(pivot, coupling, gathered, column_mask, solved_mask):
    masked = (column_mask * gathered).astype(jnp.bfloat16)
    own_rows = pivot.shape[1]
    if coupling is None:
        sums = blk_total(complex_apply(pivot, masked))
        return ((solved_mask * sums).astype(jnp.bfloat16), None)
    both = jnp.concatenate([complex_apply(pivot, masked), complex_apply(coupling, masked)], 0)
    sums = blk_total(both)
    solved = (solved_mask * sums[:own_rows]).astype(jnp.bfloat16)
    return (solved, sums[own_rows:].astype(jnp.bfloat16))


def per_device_plain(
    rhs_root,
    rhs_mid,
    rhs_leaf,
    pivot_root,
    pivot_mid,
    pivot_leaf,
    coupling_mid,
    coupling_leaf,
    front_blocks,
    child_map,
):
    cube_n = lax.axis_size("cube")
    blk_n = lax.axis_size("blk")
    cube_at = lax.axis_index("cube")
    blk_at = lax.axis_index("blk")
    slice_rows = SEPARATOR // blk_n
    slice_blocks = slice_rows // BLOCK_ROWS
    first_row = blk_at * slice_rows
    first_block = blk_at * slice_blocks
    group_mid = cube_n // 2
    group_leaf = cube_n // 4
    bits_root = cube_n.bit_length() - 1
    bits_mid = bits_root - 1
    bits_leaf = bits_root - 2
    front_mid = cube_at // group_mid
    place_mid = cube_at % group_mid
    front_leaf = cube_at // group_leaf
    place_leaf = cube_at % group_leaf
    size_root = front_blocks[0] * BLOCK_ROWS
    size_mid = front_blocks[1 + front_mid] * BLOCK_ROWS
    size_leaf = front_blocks[3 + front_leaf] * BLOCK_ROWS
    column_leaf = row_mask(first_row, slice_rows, size_leaf)
    column_mid = row_mask(first_row, slice_rows, size_mid)
    column_root = row_mask(first_row, slice_rows, size_root)
    own_leaf = pivot_leaf.shape[1]
    gathered = lax.dynamic_index_in_dim(rhs_leaf, front_leaf, 0, keepdims=False).astype(jnp.float32)
    solved_leaf, update_leaf = forward_front(
        pivot_leaf,
        coupling_leaf,
        gathered,
        column_leaf,
        row_mask(place_leaf * own_leaf, own_leaf, size_leaf),
    )
    own_mid = pivot_mid.shape[1]
    arrived = gather_bits(update_leaf, bits_mid, cube_at)
    targets = lax.dynamic_slice_in_dim(child_map, 2 + 2 * front_mid, 2, 0).reshape(-1)
    gathered = lax.dynamic_index_in_dim(rhs_mid, front_mid, 0, keepdims=False).astype(jnp.float32)
    gathered = gathered - extend_add(arrived, targets, first_block, slice_blocks)
    solved_mid, update_mid = forward_front(
        pivot_mid,
        coupling_mid,
        gathered,
        column_mid,
        row_mask(place_mid * own_mid, own_mid, size_mid),
    )
    own_root = pivot_root.shape[1]
    arrived = gather_bits(update_mid, bits_root, cube_at)
    targets = child_map[0:2].reshape(-1)
    gathered = rhs_root[0].astype(jnp.float32) - extend_add(
        arrived, targets, first_block, slice_blocks
    )
    solved_root, unused = forward_front(
        pivot_root, None, gathered, column_root, row_mask(cube_at * own_root, own_root, size_root)
    )
    total = lax.psum(complex_apply_t(pivot_root, solved_root), "cube")
    full_root = (column_root * total).astype(jnp.bfloat16)
    piece_root = slice_rows // cube_n
    answer_root = lax.dynamic_slice_in_dim(full_root, cube_at * piece_root, piece_root, 0)
    update_rows_mid = coupling_mid.shape[1]
    rows = place_mid * update_rows_mid + jnp.arange(update_rows_mid, dtype=jnp.int32)
    targets = lax.dynamic_slice_in_dim(child_map, front_mid, 1, 0).reshape(-1)
    pulled = blk_total(pick_rows(full_root, targets, rows, first_row)).astype(jnp.bfloat16)
    term = complex_apply_t(pivot_mid, solved_mid) - complex_apply_t(coupling_mid, pulled)
    piece_mid = slice_rows // group_mid
    share = halve_bits(term, bits_mid, cube_at)
    answer_mid = (row_mask(first_row + place_mid * piece_mid, piece_mid, size_mid) * share).astype(
        jnp.bfloat16
    )
    full_mid = gather_bits(answer_mid, bits_mid, cube_at)
    update_rows_leaf = coupling_leaf.shape[1]
    rows = place_leaf * update_rows_leaf + jnp.arange(update_rows_leaf, dtype=jnp.int32)
    targets = lax.dynamic_slice_in_dim(child_map, 2 + front_leaf, 1, 0).reshape(-1)
    pulled = blk_total(pick_rows(full_mid, targets, rows, first_row)).astype(jnp.bfloat16)
    term = complex_apply_t(pivot_leaf, solved_leaf) - complex_apply_t(coupling_leaf, pulled)
    piece_leaf = slice_rows // group_leaf
    share = halve_bits(term, bits_leaf, cube_at)
    answer_leaf = (
        row_mask(first_row + place_leaf * piece_leaf, piece_leaf, size_leaf) * share
    ).astype(jnp.bfloat16)
    return (answer_root[None], answer_mid[None], answer_leaf[None])

MESH = pl.DeviceIdType.MESH
VMEM = pltpu.VMEM
TILE_ROWS = 256
SLOTS = 3


class Links:
    def __init__(self, cube_n, blk_n):
        self.cube_n = cube_n
        self.blk_n = blk_n
        self.cube = lax.axis_index("cube")
        self.blk = lax.axis_index("blk")
        self.used = 0

    def bind(self, send, recv):
        self.send = send
        self.recv = recv

    def start(self, src, dst, device):
        at = self.used
        self.used += 1
        copy = pltpu.make_async_remote_copy(
            src_ref=src,
            dst_ref=dst,
            send_sem=self.send.at[at],
            recv_sem=self.recv.at[at],
            device_id=device,
            device_id_type=MESH,
        )
        copy.start()
        return copy

    def cube_peer(self, group, step):
        place = lax.rem(self.cube, group)
        other = lax.rem(place + step, group)
        return other, (self.cube - place + other, self.blk)

    def blk_peer(self, step):
        other = lax.rem(self.blk + step, self.blk_n)
        return other, (self.cube, other)

    def core(self):
        return lax.rem(self.blk, 2)

    def chip(self):
        return self.blk // 2

    def core_peer(self):
        other = 1 - self.core()
        return other, (self.cube, self.chip() * 2 + other)

    def chip_peer(self):
        other = 1 - self.chip()
        return other, (self.cube, other * 2 + self.core())

    def barrier(self, group):
        barrier = pltpu.get_barrier_semaphore()
        peers = [self.blk_peer(k)[1] for k in range(1, self.blk_n)]
        peers += [self.cube_peer(group, k)[1] for k in range(1, group)]
        for peer in peers:
            pl.semaphore_signal(barrier, inc=1, device_id=peer, device_id_type=MESH)
        pl.semaphore_wait(barrier, len(peers))


def wait_all(copies):
    for copy in copies:
        copy.wait()


def f32(value):
    return value.astype(jnp.float32)


def bf16(value):
    return value.astype(jnp.bfloat16)


def update_chain(links, src, out, got, own, group):
    copies = []
    for k in range(1, links.blk_n):
        other, device = links.blk_peer(k)
        copies.append(links.start(src.at[other], got.at[k - 1], device))
    yield
    wait_all(copies)
    total = f32(src[links.blk])
    for k in range(1, links.blk_n):
        total = total + f32(got[k - 1])
    own[...] = bf16(total)
    place = lax.rem(links.cube, group)
    out[place, links.blk] = own[...]
    copies = []
    for k in range(1, group):
        other, device = links.cube_peer(group, k)
        copies.append(links.start(own, out.at[place, links.blk], device))
    yield
    wait_all(copies)
    mine = out.at[:, links.blk]
    other, device = links.chip_peer()
    copies = [links.start(mine, mine, device)]
    other, device = links.core_peer()
    copies.append(links.start(mine, mine, device))
    yield
    wait_all(copies)
    across = out.at[:, (1 - links.chip()) * 2 + links.core()]
    copy = links.start(across, across, device)
    yield
    copy.wait()


def sum_chain(links, src, out, got_core, half, got_chip, own):
    other, device = links.core_peer()
    copy = links.start(src.at[:, other], got_core, device)
    yield
    copy.wait()
    half[...] = bf16(f32(src[:, links.core()]) + f32(got_core[...]))
    other, device = links.chip_peer()
    copy = links.start(half.at[other], got_chip, device)
    yield
    copy.wait()
    own[...] = bf16(f32(half[links.chip()]) + f32(got_chip[...]))
    out[links.chip(), links.core()] = own[...]
    place = out.at[links.chip(), links.core()]
    copy = links.start(own, place, device)
    other, device = links.core_peer()
    near = links.start(own, place, device)
    yield
    copy.wait()
    near.wait()
    place = out.at[1 - links.chip(), links.core()]
    copy = links.start(place, place, device)
    yield
    copy.wait()


def scatter_chain(links, src, out, got, group, before=0, beside=1):
    for _ in range(before):
        yield
    copies = []
    for k in range(1, group):
        other, device = links.cube_peer(group, k)
        copies.append(links.start(src.at[other], got.at[k - 1], device))
    for _ in range(beside):
        yield
    wait_all(copies)
    total = f32(src[lax.rem(links.cube, group)])
    for k in range(1, group):
        total = total + f32(got[k - 1])
    out[...] = bf16(total)


def pick_chain(links, src, out, got, mid, group, rest):
    yield from scatter_chain(links, src, mid, got, group)
    yield from sum_chain(links, mid, out, *rest)


def vm(*shape):
    return VMEM(shape, jnp.bfloat16)


def sum_scratch(rows):
    return [vm(2, rows, 128), vm(2, rows, 128), vm(rows, 128), vm(rows, 128)]


def chain_plan(kind, src, group):
    shape = src.shape
    if kind == "update":
        n, rows = shape[0], shape[1]
        return (
            (group, n, rows, 128),
            [vm(n - 1, rows, 128), vm(rows, 128)],
            n + group + 2,
            lambda L, s, o, t: update_chain(L, s, o, t[0], t[1], group),
        )
    if kind == "sum":
        return shape, sum_scratch(shape[2]), 5, lambda L, s, o, t: sum_chain(L, s, o, *t)
    if kind == "scatter":
        return (
            shape[1:],
            [vm(group - 1, *shape[1:])],
            group,
            lambda L, s, o, t: scatter_chain(L, s, o, t[0], group, 1, 4),
        )
    return (
        shape[1:],
        [vm(group - 1, *shape[1:]), vm(*shape[1:])] + sum_scratch(shape[3]),
        group + 5,
        lambda L, s, o, t: pick_chain(L, s, o, t[0], t[1], group, t[2:]),
    )


def exchange(chains, work, collective_id, cube_n, blk_n):
    plans = [chain_plan(kind, array, group) for kind, array, group in chains]
    largest = max(group for _, _, group in chains)
    n_chains = len(chains)
    arrays = [array for _, array, _ in chains]
    outs = [jax.ShapeDtypeStruct(plan[0], jnp.bfloat16) for plan in plans]
    n_copies = sum(plan[2] for plan in plans)
    scratch = [pltpu.SemaphoreType.DMA((n_copies,)), pltpu.SemaphoreType.DMA((n_copies,))]
    for plan in plans:
        scratch += plan[1]
    in_specs = [pl.BlockSpec(memory_space=VMEM)] * n_chains
    cost = None
    if work is not None:
        mode, matrix, vectors, first, rows = work
        width = matrix.shape[2]
        steps = rows // TILE_ROWS
        arrays += [matrix, vectors]
        in_specs += [pl.BlockSpec(memory_space=pl.ANY), pl.BlockSpec(memory_space=VMEM)]
        if mode == "f":
            outs.append(jax.ShapeDtypeStruct((rows, 128), jnp.bfloat16))
        else:
            outs.append(jax.ShapeDtypeStruct((128, width), jnp.float32))
        scratch += [VMEM((SLOTS, 2, TILE_ROWS, width), matrix.dtype), pltpu.SemaphoreType.DMA((SLOTS,))]

    def kernel(*refs):
        n_in = len(arrays)
        srcs, refs = refs[:n_in], refs[n_in:]
        dsts, refs = refs[: len(outs)], refs[len(outs) :]
        links = Links(cube_n, blk_n)
        links.bind(refs[0], refs[1])
        at = 2
        running = []
        for i, plan in enumerate(plans):
            count = len(plan[1])
            running.append(plan[3](links, srcs[i], dsts[i], refs[at : at + count]))
            at += count

        if work is not None:
            a_ref, v_ref = srcs[n_chains:]
            y_ref = dsts[n_chains]
            buf, sems = refs[at], refs[at + 1]

            def tile(i):
                slot = lax.rem(i, SLOTS)
                return pltpu.make_async_copy(
                    a_ref.at[:, pl.ds(first + i * TILE_ROWS, TILE_ROWS), :], buf.at[slot], sems.at[slot]
                )

            for i in range(min(SLOTS - 1, steps)):
                tile(i).start()
            if mode != "f":
                y_ref[...] = jnp.zeros_like(y_ref)

            def step(i):
                @pl.when(i + SLOTS - 1 < steps)
                def _():
                    tile(i + SLOTS - 1).start()

                tile(i).wait()
                slot = lax.rem(i, SLOTS)
                at_row = pl.ds(pl.multiple_of(i * TILE_ROWS, TILE_ROWS), TILE_ROWS)
                if mode == "f":
                    total = jnp.dot(buf[slot, 0], v_ref[0], preferred_element_type=jnp.float32)
                    total += jnp.dot(buf[slot, 1], v_ref[1], preferred_element_type=jnp.float32)
                    y_ref[at_row, :] = bf16(total)
                else:
                    both = buf[slot].reshape(2 * TILE_ROWS, width)
                    vec = jnp.concatenate([v_ref[0, i], v_ref[1, i]], axis=1)
                    y_ref[...] += jnp.dot(vec, both, preferred_element_type=jnp.float32)

        links.barrier(largest)

        def advance():
            alive = []
            for chain in running:
                try:
                    next(chain)
                    alive.append(chain)
                except StopIteration:
                    pass
            running[:] = alive

        if work is not None:
            parts = 5
            cuts = [steps * j // parts for j in range(parts + 1)]
            for lo, hi in zip(cuts, cuts[1:]):
                advance()
                if hi > lo:
                    pl.loop(lo, hi)(step)
        while running:
            advance()

    results = pl.pallas_call(
        kernel,
        out_shape=outs,
        in_specs=in_specs,
        out_specs=[pl.BlockSpec(memory_space=VMEM)] * len(outs),
        scratch_shapes=scratch,
        compiler_params=pltpu.CompilerParams(
            collective_id=collective_id, has_side_effects=True, vmem_limit_bytes=60 * 1024 * 1024
        ),
    )(*arrays)
    return results


def both_parts(vec):
    return jnp.stack([vec, rotate_parts(vec)])


def tiles_t(vec):
    parts = both_parts(vec)
    return parts.reshape(2, -1, TILE_ROWS, vec.shape[1]).transpose(0, 1, 3, 2)


def pick_blocks(piece, targets, first_block):
    blocks = piece.reshape(-1, BLOCK_ROWS, piece.shape[1])
    slots = jnp.arange(blocks.shape[0], dtype=jnp.int32)
    placing = (targets[:, None] - first_block == slots[None, :]).astype(jnp.bfloat16)
    picked = jnp.einsum("it,trd->ird", placing, blocks, preferred_element_type=jnp.float32)
    return bf16(picked).reshape(-1, piece.shape[1])


def per_device_fast(
    rhs_root,
    rhs_mid,
    rhs_leaf,
    pivot_root,
    pivot_mid,
    pivot_leaf,
    coupling_mid,
    coupling_leaf,
    front_blocks,
    child_map,
):
    cube_n = lax.axis_size("cube")
    blk_n = lax.axis_size("blk")
    cube_at = lax.axis_index("cube")
    blk_at = lax.axis_index("blk")
    slice_rows = rhs_root.shape[1]
    slice_blocks = slice_rows // BLOCK_ROWS
    first_row = blk_at * slice_rows
    first_block = blk_at * slice_blocks
    group_mid = cube_n // 2
    group_leaf = cube_n // 4
    front_mid = cube_at // group_mid
    place_mid = cube_at % group_mid
    front_leaf = cube_at // group_leaf
    place_leaf = cube_at % group_leaf
    size_root = front_blocks[0] * BLOCK_ROWS
    size_mid = front_blocks[1 + front_mid] * BLOCK_ROWS
    size_leaf = front_blocks[3 + front_leaf] * BLOCK_ROWS
    column_leaf = row_mask(first_row, slice_rows, size_leaf)
    column_mid = row_mask(first_row, slice_rows, size_mid)
    column_root = row_mask(first_row, slice_rows, size_root)
    own_leaf = pivot_leaf.shape[1]
    own_mid = pivot_mid.shape[1]
    own_root = pivot_root.shape[1]
    half_leaf = own_leaf // 2

    def by_blk(value):
        return value.reshape(blk_n, -1, 128)

    def by_core(value):
        return value.reshape(2, 2, -1, 128)

    def run(chains, work, collective_id):
        return exchange(chains, work, collective_id, cube_n, blk_n)

    gathered = f32(lax.dynamic_index_in_dim(rhs_leaf, front_leaf, 0, keepdims=False))
    masked_leaf = bf16(column_leaf * gathered)
    update = bf16(complex_apply(coupling_leaf, masked_leaf))
    vec_leaf = both_parts(masked_leaf)
    arrived, solved_low = run(
        [("update", by_blk(update), group_mid)], ("f", pivot_leaf, vec_leaf, 0, half_leaf), 0
    )
    targets = lax.dynamic_slice_in_dim(child_map, 2 + 2 * front_mid, 2, 0).reshape(-1)
    gathered = f32(lax.dynamic_index_in_dim(rhs_mid, front_mid, 0, keepdims=False))
    gathered = gathered - extend_add(arrived.reshape(-1, 128), targets, first_block, slice_blocks)
    masked_mid = bf16(column_mid * gathered)
    update = bf16(complex_apply(coupling_mid, masked_mid))
    arrived, solved_low, solved_mid = run(
        [("update", by_blk(update), cube_n), ("sum", by_core(solved_low), 1)],
        ("f", pivot_mid, both_parts(masked_mid), 0, own_mid),
        1,
    )
    targets = child_map[0:2].reshape(-1)
    gathered = f32(rhs_root[0]) - extend_add(
        arrived.reshape(-1, 128), targets, first_block, slice_blocks
    )
    masked_root = bf16(column_root * gathered)
    solved_root = bf16(complex_apply(pivot_root, masked_root))
    solved_root, solved_mid, solved_high = run(
        [("sum", by_core(solved_root), 1), ("sum", by_core(solved_mid), 1)],
        ("f", pivot_leaf, vec_leaf, half_leaf, own_leaf - half_leaf),
        2,
    )
    solved_root = bf16(
        row_mask(cube_at * own_root, own_root, size_root) * f32(solved_root.reshape(-1, 128))
    )
    solved_mid = bf16(
        row_mask(place_mid * own_mid, own_mid, size_mid) * f32(solved_mid.reshape(-1, 128))
    )
    part_root = bf16(column_root * complex_apply_t(pivot_root, solved_root))
    targets = child_map[0:2].reshape(-1)
    picked = pick_blocks(part_root, targets, first_block)
    pulled, solved_high, term = run(
        [
            ("pick", picked.reshape(cube_n, 2, 2, -1, 128), cube_n),
            ("sum", by_core(solved_high), 1),
        ],
        ("t", pivot_mid, tiles_t(solved_mid), 0, own_mid),
        3,
    )
    first_leaf = place_leaf * own_leaf
    mask_low = row_mask(first_leaf, half_leaf, size_leaf)
    mask_high = row_mask(first_leaf + half_leaf, own_leaf - half_leaf, size_leaf)
    tiles_low = tiles_t(bf16(mask_low * f32(solved_low.reshape(-1, 128))))
    tiles_high = tiles_t(bf16(mask_high * f32(solved_high.reshape(-1, 128))))
    tiles_leaf = jnp.concatenate([tiles_low, tiles_high], 1)
    term = term.T - complex_apply_t(coupling_mid, pulled.reshape(-1, 128))
    part_mid = bf16(column_mid * term)
    targets = lax.dynamic_slice_in_dim(child_map, 2 + 2 * front_mid, 2, 0).reshape(-1)
    picked = pick_blocks(part_mid, targets, first_block)
    pulled, answer_root, answer_mid, term = run(
        [
            ("pick", picked.reshape(group_mid, 2, 2, -1, 128), group_mid),
            ("scatter", part_root.reshape(cube_n, -1, 128), cube_n),
            ("scatter", part_mid.reshape(group_mid, -1, 128), group_mid),
        ],
        ("t", pivot_leaf, tiles_leaf, 0, own_leaf),
        4,
    )
    term = term.T - complex_apply_t(coupling_leaf, pulled.reshape(-1, 128))
    part_leaf = bf16(column_leaf * term)
    (answer_leaf,) = run(
        [("scatter", part_leaf.reshape(group_leaf, -1, 128), group_leaf)], None, 5
    )
    return (answer_root[None], answer_mid[None], answer_leaf[None])


def per_device(*args):
    cube_n = lax.axis_size("cube")
    blk_n = lax.axis_size("blk")
    pivot_root, pivot_mid, pivot_leaf, coupling_mid = args[3], args[4], args[5], args[6]
    fits = (
        blk_n == 4
        and cube_n % 4 == 0
        and args[0].shape[2] == 128
        and coupling_mid.shape[1] % (16 * blk_n) == 0
        and pivot_root.shape[1] % (16 * blk_n) == 0
        and pivot_leaf.shape[1] % (32 * blk_n) == 0
        and pivot_mid.shape[1] % TILE_ROWS == 0
        and pivot_leaf.shape[1] % (2 * TILE_ROWS) == 0
    )
    return per_device_fast(*args) if fits else per_device_plain(*args)


def solution(mesh):
    in_specs = (
        P(None, "blk", None),
        P(None, "blk", None),
        P(None, "blk", None),
        P(None, "cube", "blk"),
        P(None, "cube", "blk"),
        P(None, "cube", "blk"),
        P(None, "cube", "blk"),
        P(None, "cube", "blk"),
        P(),
        P(),
    )
    out_specs = (P("blk", "cube", None), P("blk", "cube", None), P("blk", "cube", None))
    return jax.shard_map(
        per_device, mesh=mesh, in_specs=in_specs, out_specs=out_specs, check_vma=False
    )
```
